32 devices in a mesh: dp: 2 (over x), expert: 16 (over z, y, core).
Axes of the slice: x: 2, y: 2, z: 4, core: 2. Of those that a mesh axis runs over, the one named last changes fastest.
Arguments:
- tokens: bfloat16 [2048, 4096], P('expert', 'dp'), may hold values from -6 to 6
- expert_ids: int32 [2048, 8], P('expert'), may hold values from 0 to 15, all different within a row; in each aligned block of 128 rows (0 to 127, 128 to 255, ...) at most 96 rows name the same one
- gates: float32 [2048, 8], P('expert'), may hold values from 0.1 to 0.6
- cotangent: bfloat16 [2048, 4096], P('expert', 'dp'), may hold values from -0.59765625 to 0.59765625
- partner: int32 [16], replicated, may hold values from -1 to 15, as said below
- w_gate: bfloat16 [16, 4096, 1024], P('expert', 'dp'), may hold values from -0.09375 to 0.09375
- w_up: bfloat16 [16, 4096, 1024], P('expert', 'dp'), may hold values from -0.09375 to 0.09375
- w_down: bfloat16 [16, 1024, 4096], P('expert', None, 'dp'), may hold values from -0.1875 to 0.1875
Outputs:
- mixed: bfloat16 [2048, 4096], P('expert', 'dp')
- grad_tokens: bfloat16 [2048, 4096], P('expert', 'dp')
- grad_gates: float32 [2048, 8], P('expert')
- grad_gate_w: bfloat16 [16, 4096, 1024], P('expert', 'dp')
- grad_up_w: bfloat16 [16, 4096, 1024], P('expert', 'dp')
- grad_down_w: bfloat16 [16, 1024, 4096], P('expert', None, 'dp')
The draws below stay inside these ranges and needn't reach their ends.
Inputs may be any that keep to these rules, and one draw needn't show every extreme that they name: `expert_ids`: each row names 8 different experts. In each aligned block of 128 rows no expert is named more than 64 + 32 times, and in some block some expert is named exactly that many times. Exactly 8 entries are -1. The others name distinct experts, and for each such expert e, partner[e] is -1.
All inputs are finite; a program needn't handle non-finite values.
Results may differ from the reference program's by a relative error of at most 0.023.
Values may be sent and summed in bfloat16 or wider, within the bound.
A program may use at most 192 MiB of HBM per device.

```python
import math
import jax
import jax.numpy as jnp
import numpy as np
from jax import lax

D = 4096
H = 1024
K = 8
TOK_DEV = 128
EXPERTS = 16
TOKENS = 2048
CAP = 64
SPILL = 32
N_DP = 2
N_EXPERT = 16


def draw_partner(key, part):
    order = jax.random.permutation(key, N_EXPERT).astype(jnp.int32)
    last = N_EXPERT - 1
    where_last = jnp.argmax((order == last).astype(jnp.int32)).astype(jnp.int32)
    first = order[0]
    order = order.at[where_last].set(first).at[0].set(last)
    half = N_EXPERT // 2
    return jnp.full((N_EXPERT,), -1, jnp.int32).at[order[half:]].set(order[:half])


def steps_of(rng, extent, shards, smallest, largest):
    def one(dim, parts):
        steps = jax.random.uniform(jax.random.fold_in(jax.random.fold_in(rng, 6), dim), (parts,), jnp.float32, smallest / len(shards), largest / len(shards))
        return jnp.repeat(jnp.exp(steps), extent[dim] // parts).reshape((-1,) + (1,) * (len(extent) - dim - 1))

    level = one(*shards[0])
    for cut in shards[1:]:
        level = level * one(*cut)
    return level


def deal_out(stream_key, own, number, rows, count, top, bound, slope):
    order = jax.random.permutation(stream_key, count)
    packed, common = portions_of(count, rows * top, bound, slope, True), portions_of(count, rows * top, bound, slope, False)
    places = jnp.arange(count)

    def named(sizes, rotation):
        used = int((sizes > 0).sum())
        fixed = max(1, used // 4)
        passed = fixed + (places - fixed + rotation * (used - fixed)) % max(1, count - fixed)
        return jnp.zeros((count,), jnp.int32).at[order[jnp.where(places < fixed, places, passed)]].set(jnp.asarray(sizes, jnp.int32))

    sizes = jnp.where(number % 4 == 0, named(packed, number // 4), named(common, number - number // 4 - 1))
    mixed = jax.random.permutation(jax.random.fold_in(own, 3), count)
    donor, taker = mixed[0:count // 2 * 2:2], mixed[1:count // 2 * 2:2]
    slack = jnp.minimum(sizes[donor] - 1, bound - sizes[taker]) // 2
    slack = jnp.where((donor == order[0]) | (taker == order[0]) | (sizes[taker] == 0), 0, jnp.maximum(slack, 0))
    passed = jax.random.randint(jax.random.fold_in(own, 4), (count // 2,), 0, 1 << 20) % (slack + 1)
    sizes = sizes.at[donor].add(-passed).at[taker].add(passed)
    items = jnp.searchsorted(jnp.cumsum(sizes), jnp.arange(rows * top), side="right").astype(jnp.int32)
    listing = items.reshape(top, rows).T
    listing = listing[jax.random.permutation(jax.random.fold_in(own, 1), rows)]
    rotation = jax.random.randint(jax.random.fold_in(own, 2), (rows, 1), 0, top)
    return jnp.take_along_axis(listing, (jnp.arange(top)[None, :] + rotation) % top, axis=1)


def portions_of(number_of, total, reach, lean, full):
    portions = [(1 << 20) // math.isqrt(rank ** lean) + 1 for rank in range(1, number_of + 1)]
    largest = reach if full else min(reach, max(-(-total // number_of), total * portions[0] // sum(portions)))
    least = 1 if total - largest >= number_of - 1 else 0
    holding, surplus = [largest] + [least] * (number_of - 1), total - largest - least * (number_of - 1)
    while surplus > 0:
        candidates = [i for i in range(1, number_of) if holding[i] < largest] or [i for i in range(1, number_of) if holding[i] < reach]
        pool, left = sum([portions[i] for i in candidates]), surplus
        for i in candidates:
            addition = min(reach - holding[i], max(1, left * portions[i] // pool), surplus)
            holding[i] = holding[i] + addition
            surplus = surplus - addition
    return np.array(holding)


def scatter_about(own_key, extent, deviation, most, cuts=(), kind=jnp.bfloat16):
    array = jax.random.normal(own_key, extent, jnp.float32) * deviation
    if len(cuts) > 0:
        array = steps_of(own_key, extent, cuts, -0.22, 0.18) * array
    return jnp.clip(array, min=-most, max=most).astype(kind)


def setup_inputs(seed: int = 0) -> dict:
    splits = jax.random.split(jax.random.key(seed), 9)
    tokens = scatter_about(splits[0], (TOKENS, D), 1.0, 6.0, ((0, 16), (1, 2)))
    expert_ids_keys = jax.random.split(jax.random.fold_in(splits[1], 1), TOKENS // TOK_DEV)
    expert_ids_turns = jax.random.permutation(jax.random.fold_in(splits[1], 3), TOKENS // TOK_DEV)
    expert_ids = jax.vmap(lambda own, number: deal_out(jax.random.fold_in(splits[1], 2), own, number, TOK_DEV, EXPERTS, K, CAP + SPILL, 2))(expert_ids_keys, expert_ids_turns).reshape((TOKENS, K))
    gates = jnp.clip(0.1 + 0.5 * jax.random.uniform(splits[2], (TOKENS, K), jnp.float32) ** steps_of(splits[2], (TOKENS, K), ((0, 16),), -0.2, 0.2), 0.1, 0.6)
    cotangent = scatter_about(splits[3], (TOKENS, D), 0.1, 0.59765625, ((0, 16), (1, 2)))
    partner = draw_partner(jax.random.fold_in(splits[8], 71), 0)
    w_gate = scatter_about(splits[5], (EXPERTS, D, H), D ** -0.5, 0.09375, ((0, 16), (1, 2)))
    w_up = scatter_about(splits[6], (EXPERTS, D, H), D ** -0.5, 0.09375, ((0, 16), (1, 2)))
    w_down = scatter_about(splits[7], (EXPERTS, H, D), H ** -0.5, 0.1875, ((0, 16), (2, 2)))
    return dict(tokens=tokens, expert_ids=expert_ids, gates=gates, cotangent=cotangent, partner=partner, w_gate=w_gate, w_up=w_up, w_down=w_down)


def slot_ranks(expert_ids):
    blocks = expert_ids.reshape(N_EXPERT, TOK_DEV * K)
    labels = jnp.arange(EXPERTS, dtype=jnp.int32)
    onehot = (blocks[:, :, None] == labels[None, None, :]).astype(jnp.int32)
    counted = jnp.cumsum(onehot, axis=1) - 1
    return lax.optimization_barrier(jnp.sum(counted * onehot, axis=2)).reshape(TOKENS, K)

def piece_sums(left, weight):
    pieces = left.astype(jnp.float32).reshape(left.shape[0], N_DP, D // N_DP)
    wpieces = weight.astype(jnp.float32).reshape(N_DP, D // N_DP, H)
    terms = jnp.einsum('rsd,sdh->rsh', pieces, wpieces).astype(jnp.bfloat16)
    terms = lax.optimization_barrier(terms)
    return lax.optimization_barrier(jnp.sum(terms.astype(jnp.float32), axis=1))

def piece_sums_down(left, weight):
    pieces = left.astype(jnp.float32).reshape(left.shape[0], N_DP, D // N_DP)
    wpieces = weight.astype(jnp.float32).reshape(H, N_DP, D // N_DP)
    terms = jnp.einsum('rsd,hsd->rsh', pieces, wpieces).astype(jnp.bfloat16)
    terms = lax.optimization_barrier(terms)
    return lax.optimization_barrier(jnp.sum(terms.astype(jnp.float32), axis=1))

def split_grad(left, right):
    home_count = N_EXPERT * CAP
    home_sum = jnp.dot(left[:home_count].T, right[:home_count], preferred_element_type=jnp.float32)
    copy_sum = jnp.dot(left[home_count:].T, right[home_count:], preferred_element_type=jnp.float32).astype(jnp.bfloat16)
    copy_sum = lax.optimization_barrier(copy_sum)
    return (home_sum + copy_sum.astype(jnp.float32)).astype(jnp.bfloat16)

def reference(tokens, expert_ids, gates, cotangent, partner, w_gate, w_up, w_down):
    rank = slot_ranks(expert_ids)
    labels = jnp.arange(EXPERTS, dtype=jnp.int32)
    hosted = lax.optimization_barrier(jnp.sum((partner[:, None] == labels[None, :]).astype(jnp.int32), axis=0))
    pair_hosted = hosted[expert_ids]
    block = (jnp.arange(TOKENS, dtype=jnp.int32) // TOK_DEV)[:, None]
    home_count = N_EXPERT * CAP
    all_rows = N_EXPERT * (CAP + SPILL)
    dump = EXPERTS * all_rows
    home_place = expert_ids * all_rows + block * CAP + rank
    spill_place = expert_ids * all_rows + home_count + block * SPILL + rank - CAP
    place = jnp.where(rank < CAP, home_place, jnp.where(pair_hosted > 0, spill_place, dump))
    sentinel = TOKENS * K
    table = jnp.full((dump + 1,), sentinel, jnp.int32)
    table = table.at[place.reshape(-1)].set(jnp.arange(TOKENS * K, dtype=jnp.int32))
    table = table[:dump].reshape(EXPERTS, all_rows)
    tok_pad = jnp.concatenate([tokens, jnp.zeros((1, D), jnp.bfloat16)], axis=0)
    cot_pad = jnp.concatenate([cotangent, jnp.zeros((1, D), jnp.bfloat16)], axis=0)
    gate_pad = jnp.concatenate([gates.reshape(-1), jnp.zeros((1,), jnp.float32)], axis=0)

    def expert_step(carry, inputs):
        mixed, grad_tokens, grad_gates = carry
        slots, wg, wu, wd = inputs
        owner = slots // K
        xs = tok_pad[owner]
        weight_of = gate_pad[slots]
        cot_rows = cot_pad[owner].astype(jnp.float32)
        dout = (weight_of[:, None] * cot_rows).astype(jnp.bfloat16)
        gate_pre = piece_sums(xs, wg)
        up_pre = piece_sums(xs, wu)
        dhid = piece_sums_down(dout, wd)
        sig = jax.nn.sigmoid(gate_pre)
        act = gate_pre * sig
        hid = (act * up_pre).astype(jnp.bfloat16)
        dup = (dhid * act).astype(jnp.bfloat16)
        dgate = (dhid * up_pre * sig * (1.0 + gate_pre * (1.0 - sig))).astype(jnp.bfloat16)
        out = jnp.dot(hid, wd, preferred_element_type=jnp.float32).astype(jnp.bfloat16)
        dxs = (jnp.dot(dgate, wg.T, preferred_element_type=jnp.float32) + jnp.dot(dup, wu.T, preferred_element_type=jnp.float32)).astype(jnp.bfloat16)
        grad_down = split_grad(hid, dout)
        grad_gate = split_grad(xs, dgate)
        grad_up = split_grad(xs, dup)
        outf = out.astype(jnp.float32)
        mixed = mixed.at[owner].add(weight_of[:, None] * outf)
        grad_tokens = grad_tokens.at[owner].add(dxs.astype(jnp.float32))
        grad_gates = grad_gates.at[slots].set(lax.optimization_barrier(jnp.sum(cot_rows * outf, axis=1)))
        return ((mixed, grad_tokens, grad_gates), (grad_gate, grad_up, grad_down))
    start = (jnp.zeros((TOKENS + 1, D), jnp.float32), jnp.zeros((TOKENS + 1, D), jnp.float32), jnp.zeros((TOKENS * K + 1,), jnp.float32))
    final, grads = lax.scan(expert_step, start, (table, w_gate, w_up, w_down))
    mixed, grad_tokens, grad_gates = final
    return (mixed[:TOKENS].astype(jnp.bfloat16), grad_tokens[:TOKENS].astype(jnp.bfloat16), grad_gates[:TOKENS * K].reshape(TOKENS, K), grads[0], grads[1], grads[2])
```

```python
import jax
import jax.numpy as jnp
from jax import lax
from jax.sharding import PartitionSpec as P


def dot(left, right, dims):
    return lax.dot_general(left, right, (dims, ((), ())), preferred_element_type=jnp.float32)


def pick(onehot, values):
    rows = lax.dot_general(
        onehot, values, (((2,), (1,)), ((0,), (0,))), preferred_element_type=jnp.float32
    )
    return rows.astype(jnp.bfloat16).reshape(-1, values.shape[2])


def local(tokens, expert_ids, gates, cotangent, partner, w_gate, w_up, w_down):
    n_exp = lax.axis_size("expert")
    n_dp = lax.axis_size("dp")
    me = lax.axis_index("expert")
    rows, width = tokens.shape
    top = expert_ids.shape[1]
    cap = rows * top // n_exp
    slots = cap + cap // 2
    own_gate, own_up, own_down = w_gate[0], w_up[0], w_down[0]

    small = jnp.concatenate([expert_ids.T.astype(jnp.float32), gates.T], axis=0)
    small = lax.all_gather(small, "expert", axis=0, tiled=False)
    all_x = lax.all_gather(tokens, "expert", axis=0, tiled=False)
    all_c = lax.all_gather(cotangent, "expert", axis=0, tiled=False)

    hit = small[:, :top] == me.astype(jnp.float32)
    present = jnp.any(hit, axis=1)
    token_gate = jnp.sum(jnp.where(hit, small[:, top:], 0.0), axis=1)
    order = jnp.arange(rows)
    earlier = (order[:, None] < order[None, :]).astype(jnp.bfloat16)
    rank = dot(present.astype(jnp.bfloat16), earlier, ((1,), (0,))).astype(jnp.int32)
    limit = jnp.where(jnp.any(partner == me), slots, cap)
    taken = jnp.logical_and(present, rank < limit)
    place = jnp.where(taken, rank, -1)
    match = place[:, None, :] == jnp.arange(slots)[None, :, None]
    onehot = match.astype(jnp.bfloat16)
    slot_gate = jnp.sum(jnp.where(match, token_gate[:, None, :], 0.0), axis=2).reshape(-1, 1)
    back = (jnp.arange(slots)[None, None, :] == place[:, :, None]).astype(jnp.bfloat16)

    xs = pick(onehot, all_x)
    pre_g = dot(xs, own_gate, ((1,), (0,))).astype(jnp.bfloat16)
    pre_u = dot(xs, own_up, ((1,), (0,))).astype(jnp.bfloat16)
    cs = pick(onehot, all_c)
    pre_d = dot(cs, own_down, ((1,), (1,))).astype(jnp.bfloat16)

    if n_dp == 2:
        swap = [(0, 1), (1, 0)]

        def summed(part):
            other = lax.ppermute(part, "dp", swap)
            return part.astype(jnp.float32) + other.astype(jnp.float32)

        def full(part):
            return part
    else:

        def summed(part):
            part = lax.psum_scatter(part, "dp", scatter_dimension=1, tiled=True)
            return part.astype(jnp.float32)

        def full(part):
            return lax.all_gather(part, "dp", axis=1, tiled=True)

    gate_pre = summed(pre_g)
    up_pre = summed(pre_u)
    sig = jax.nn.sigmoid(gate_pre)
    act = gate_pre * sig
    hid = act * up_pre
    scaled_hid = full((slot_gate * hid).astype(jnp.bfloat16))

    def send_home(slot_rows):
        parts = pick(back, slot_rows.reshape(n_exp, slots, width))
        return lax.psum_scatter(parts, "expert", scatter_dimension=0, tiled=True)

    out = dot(scaled_hid, own_down, ((1,), (0,))).astype(jnp.bfloat16)
    mixed = send_home(out)

    raw = summed(pre_d)
    dhid = slot_gate * raw
    dup = full((dhid * act).astype(jnp.bfloat16))
    dgate = full((dhid * up_pre * sig * (1.0 + gate_pre * (1.0 - sig))).astype(jnp.bfloat16))
    slot_terms = jnp.sum(hid * raw, axis=1).reshape(n_exp, 1, slots)
    dx = (dot(dgate, own_gate, ((1,), (1,))) + dot(dup, own_up, ((1,), (1,)))).astype(jnp.bfloat16)
    grad_tokens = send_home(dx)

    mine = place[:, :, None] == jnp.arange(slots)[None, None, :]
    terms = jnp.sum(jnp.where(mine, slot_terms, 0.0), axis=2)
    terms = lax.all_to_all(terms, "expert", split_axis=0, concat_axis=0, tiled=True)
    labels = jnp.arange(n_exp, dtype=jnp.int32)
    chosen = expert_ids.T[None, :, :] == labels[:, None, None]
    grad_gates = jnp.sum(jnp.where(chosen, terms[:, None, :], 0.0), axis=0).T
    if n_dp != 2:
        grad_gates = lax.psum(grad_gates, "dp")

    grad_down = dot(scaled_hid, cs, ((0,), (0,))).astype(jnp.bfloat16)
    grad_up = dot(xs, dup, ((0,), (0,))).astype(jnp.bfloat16)
    grad_gate = dot(xs, dgate, ((0,), (0,))).astype(jnp.bfloat16)
    return (mixed, grad_tokens, grad_gates, grad_gate[None], grad_up[None], grad_down[None])


def solution(mesh):
    placed = (
        P("expert", "dp"),
        P("expert", None),
        P("expert", None),
        P("expert", "dp"),
        P(),
        P("expert", "dp", None),
        P("expert", "dp", None),
        P("expert", None, "dp"),
    )
    return jax.shard_map(
        local,
        mesh=mesh,
        in_specs=placed,
        out_specs=(
            P("expert", "dp"),
            P("expert", "dp"),
            P("expert", None),
            P("expert", "dp", None),
            P("expert", "dp", None),
            P("expert", None, "dp"),
        ),
        check_vma=False,
    )
```

```python
import jax
import jax.numpy as jnp
from jax import lax
from jax.sharding import PartitionSpec as P


def dot(left, right, dims):
    return lax.dot_general(left, right, (dims, ((), ())), preferred_element_type=jnp.float32)


def pick(onehot, values):
    rows = lax.dot_general(
        onehot, values, (((2,), (1,)), ((0,), (0,))), preferred_element_type=jnp.float32
    )
    return rows.astype(jnp.bfloat16).reshape(-1, values.shape[2])


def local(tokens, expert_ids, gates, cotangent, partner, w_gate, w_up, w_down):
    n_exp = lax.axis_size("expert")
    n_dp = lax.axis_size("dp")
    me = lax.axis_index("expert")
    rows, width = tokens.shape
    top = expert_ids.shape[1]
    cap = rows * top // n_exp
    slots = cap + cap // 2
    own_gate, own_up, own_down = w_gate[0], w_up[0], w_down[0]

    small = jnp.concatenate([expert_ids.T.astype(jnp.float32), gates.T], axis=0)
    small = lax.all_gather(small, "expert", axis=0, tiled=False)
    all_x = lax.all_gather(tokens, "expert", axis=0, tiled=False)
    later, all_x = lax.optimization_barrier((cotangent, all_x))
    all_c = lax.all_gather(later, "expert", axis=0, tiled=False)

    hit = small[:, :top] == me.astype(jnp.float32)
    present = jnp.any(hit, axis=1)
    token_gate = jnp.sum(jnp.where(hit, small[:, top:], 0.0), axis=1)
    order = jnp.arange(rows)
    earlier = (order[:, None] < order[None, :]).astype(jnp.bfloat16)
    rank = dot(present.astype(jnp.bfloat16), earlier, ((1,), (0,))).astype(jnp.int32)
    limit = jnp.where(jnp.any(partner == me), slots, cap)
    taken = jnp.logical_and(present, rank < limit)
    place = jnp.where(taken, rank, -1)
    match = place[:, None, :] == jnp.arange(slots)[None, :, None]
    onehot = match.astype(jnp.bfloat16)
    slot_gate = jnp.sum(jnp.where(match, token_gate[:, None, :], 0.0), axis=2).reshape(-1, 1)
    back = (jnp.arange(slots)[None, None, :] == place[:, :, None]).astype(jnp.bfloat16)

    xs = pick(onehot, all_x)
    pre_g = dot(xs, own_gate, ((1,), (0,))).astype(jnp.bfloat16)
    pre_u = dot(xs, own_up, ((1,), (0,))).astype(jnp.bfloat16)
    cs = pick(onehot, all_c)
    pre_d = dot(cs, own_down, ((1,), (1,))).astype(jnp.bfloat16)

    if n_dp == 2:
        swap = [(0, 1), (1, 0)]

        def exchange(part):
            return (part, lax.ppermute(part, "dp", swap))

        def summed(both):
            return both[0].astype(jnp.float32) + both[1].astype(jnp.float32)

        def full(part):
            return part
    else:

        def exchange(part):
            return (lax.psum_scatter(part, "dp", scatter_dimension=1, tiled=True),)

        def summed(both):
            return both[0].astype(jnp.float32)

        def full(part):
            return lax.all_gather(part, "dp", axis=1, tiled=True)

    sum_g = exchange(pre_g)
    sum_u = exchange(pre_u)
    sum_d = exchange(pre_d)
    sum_g, sum_u, _ = lax.optimization_barrier((sum_g, sum_u, pre_d))
    gate_pre = summed(sum_g)
    up_pre = summed(sum_u)
    sig = jax.nn.sigmoid(gate_pre)
    act = gate_pre * sig
    hid = act * up_pre
    scaled_hid = full((slot_gate * hid).astype(jnp.bfloat16))

    def to_tokens(slot_rows):
        return pick(back, slot_rows.reshape(n_exp, slots, width))

    def send_home(parts):
        return lax.psum_scatter(parts, "expert", scatter_dimension=0, tiled=True)

    out = dot(scaled_hid, own_down, ((1,), (0,))).astype(jnp.bfloat16)
    out_parts = to_tokens(out)
    mixed = send_home(out_parts)

    sum_d, sum_g, sum_u, _ = lax.optimization_barrier((sum_d, sum_g, sum_u, out_parts))
    gate_pre = summed(sum_g)
    up_pre = summed(sum_u)
    sig = jax.nn.sigmoid(gate_pre)
    act = gate_pre * sig
    hid = act * up_pre
    raw = summed(sum_d)
    dhid = slot_gate * raw
    dup = full((dhid * act).astype(jnp.bfloat16))
    dgate = full((dhid * up_pre * sig * (1.0 + gate_pre * (1.0 - sig))).astype(jnp.bfloat16))
    slot_terms = jnp.sum(hid * raw, axis=1).reshape(n_exp, 1, slots)
    dx = (dot(dgate, own_gate, ((1,), (1,))) + dot(dup, own_up, ((1,), (1,)))).astype(jnp.bfloat16)
    grad_tokens = send_home(to_tokens(dx))

    mine = place[:, :, None] == jnp.arange(slots)[None, None, :]
    terms = jnp.sum(jnp.where(mine, slot_terms, 0.0), axis=2)
    terms = lax.all_to_all(terms, "expert", split_axis=0, concat_axis=0, tiled=True)
    labels = jnp.arange(n_exp, dtype=jnp.int32)
    chosen = expert_ids.T[None, :, :] == labels[:, None, None]
    grad_gates = jnp.sum(jnp.where(chosen, terms[:, None, :], 0.0), axis=0).T
    if n_dp != 2:
        grad_gates = lax.psum(grad_gates, "dp")

    grad_down = dot(scaled_hid, cs, ((0,), (0,))).astype(jnp.bfloat16)
    grad_up = dot(xs, dup, ((0,), (0,))).astype(jnp.bfloat16)
    grad_gate = dot(xs, dgate, ((0,), (0,))).astype(jnp.bfloat16)
    return (mixed, grad_tokens, grad_gates, grad_gate[None], grad_up[None], grad_down[None])


def solution(mesh):
    placed = (
        P("expert", "dp"),
        P("expert", None),
        P("expert", None),
        P("expert", "dp"),
        P(),
        P("expert", "dp", None),
        P("expert", "dp", None),
        P("expert", None, "dp"),
    )
    return jax.shard_map(
        local,
        mesh=mesh,
        in_specs=placed,
        out_specs=(
            P("expert", "dp"),
            P("expert", "dp"),
            P("expert", None),
            P("expert", "dp", None),
            P("expert", "dp", None),
            P("expert", None, "dp"),
        ),
        check_vma=False,
    )
```
